512 devices in a mesh: expert: 128 (over z, y, core), dp: 4 (over x).
Axes of the slice: x: 4, y: 8, z: 8, core: 2. Of those that a mesh axis runs over, the one named last changes fastest.
Arguments:
- inputs: bfloat16 [65536, 256], P(('expert', 'dp')), may hold values from -4 to 4
- out_grad: bfloat16 [65536, 2048], P(('expert', 'dp')), may hold values from -6 to 6
- route: int32 [65536, 1], P(('expert', 'dp')), may hold values from 0 to 31; in each aligned block of 128 rows (0 to 127, 128 to 255, ...) at most 8 rows name the same one
- coef: bfloat16 [128, 256, 8, 512], P('expert', 'dp'), may hold values from -0.125 to 0.125
- first_moment: bfloat16 [128, 256, 8, 512], P('expert', 'dp'), may hold values from -15 to 15
- second_moment: bfloat16 [128, 256, 8, 512], P('expert', 'dp'), may hold values from 1 to 100
Outputs:
- input_grad: bfloat16 [65536, 256], P(('expert', 'dp'))
- new_coef: bfloat16 [128, 256, 8, 512], P('expert', 'dp')
- new_first: bfloat16 [128, 256, 8, 512], P('expert', 'dp')
- new_second: bfloat16 [128, 256, 8, 512], P('expert', 'dp')
The draws below stay inside these ranges and needn't reach their ends.
Inputs may be any that keep to these rules, and one draw needn't show every extreme that they name: `route`: each row names one expert. Among the rows of one device no expert is named by more than 8 rows, and on some device one expert is named by exactly 8 rows.
All inputs are finite; a program needn't handle non-finite values.
Results may differ from the reference program's by a relative error of at most 0.0085.
Values may be sent and summed in bfloat16 or wider, within the bound.
No kernel may reach another device: no remote copies, remote signals or barrier semaphores. Data moves between devices by JAX's collectives and lax.ppermute only.
A program may use at most 64 MiB of HBM per device.

```python
import math
import jax
import jax.numpy as jnp
import numpy as np
from jax import lax

IN = 256
OUT = 2048
NB = 8
SPLIT = 4
ROWS_DEV = 128
COLS = 512
EXPERTS = 32
CAP = 8
ROWS = 65536
GROUPS = 128
N_EXPERT = 128
N_DP = 4


def block_levels(own_key, dims, pieces, least, top_value):
    factor_of = 1.0
    for position, parts in pieces:
        steps = jax.random.uniform(jax.random.fold_in(jax.random.fold_in(own_key, 6), position), (parts,), jnp.float32, least / len(pieces), top_value / len(pieces))
        factor_of = factor_of * jnp.repeat(jnp.exp(steps), dims[position] // parts).reshape((-1,) + (1,) * (len(dims) - 1 - position))
    return factor_of


def shared_out(own_key, own, number, rows, number_of, top, bound, slope):
    sequence = jax.random.permutation(own_key, number_of)
    heavy_load, usual = portions_of(number_of, rows * top, bound, slope, True), portions_of(number_of, rows * top, bound, slope, False)
    places = jnp.arange(number_of)

    def named(tallies, rotation):
        used = int((tallies > 0).sum())
        fixed = max(1, used // 4)
        passed = fixed + (places - fixed + rotation * (used - fixed)) % max(1, number_of - fixed)
        return jnp.zeros((number_of,), jnp.int32).at[sequence[jnp.where(places < fixed, places, passed)]].set(jnp.asarray(tallies, jnp.int32))

    tallies = jnp.where(number % 4 == 0, named(heavy_load, number // 4), named(usual, number - number // 4 - 1))
    mixed = jax.random.permutation(jax.random.fold_in(own, 3), number_of)
    donor, taker = mixed[0:number_of // 2 * 2:2], mixed[1:number_of // 2 * 2:2]
    slack = jnp.minimum(tallies[donor] - 1, bound - tallies[taker]) // 2
    slack = jnp.where((donor == sequence[0]) | (taker == sequence[0]) | (tallies[taker] == 0), 0, jnp.maximum(slack, 0))
    passed = jax.random.randint(jax.random.fold_in(own, 4), (number_of // 2,), 0, 1 << 20) % (slack + 1)
    tallies = tallies.at[donor].add(-passed).at[taker].add(passed)
    items = jnp.searchsorted(jnp.cumsum(tallies), jnp.arange(rows * top), side="right").astype(jnp.int32)
    table = items.reshape(top, rows).T
    table = table[jax.random.permutation(jax.random.fold_in(own, 1), rows)]
    rotation = jax.random.randint(jax.random.fold_in(own, 2), (rows, 1), 0, top)
    return jnp.take_along_axis(table, (jnp.arange(top)[None, :] + rotation) % top, axis=1)


def portions_of(amount, total, reach, lean, full):
    loads = [(1 << 20) // math.isqrt(grade ** lean) + 1 for grade in range(1, amount + 1)]
    largest = reach if full else min(reach, max(-(-total // amount), total * loads[0] // sum(loads)))
    least = 1 if total - largest >= amount - 1 else 0
    given, spare = [largest] + [least] * (amount - 1), total - largest - least * (amount - 1)
    while spare > 0:
        free = [i for i in range(1, amount) if given[i] < largest] or [i for i in range(1, amount) if given[i] < reach]
        mass, left = sum([loads[i] for i in free]), spare
        for i in free:
            extra = min(reach - given[i], max(1, left * loads[i] // mass), spare)
            given[i] = given[i] + extra
            spare = spare - extra
    return np.array(given)


def noise(key, extent, spread, limit, cuts=(), held_as=jnp.bfloat16):
    values = jax.random.normal(key, extent, jnp.float32) * spread
    if len(cuts) > 0:
        values = block_levels(key, extent, cuts, -0.22, 0.18) * values
    return jnp.clip(values, min=-limit, max=limit).astype(held_as)


def setup_inputs(seed: int = 0) -> dict:
    streams_of = jax.random.split(jax.random.key(seed), 7)
    inputs = noise(streams_of[0], (ROWS, IN), 1.2, 4.0, ((0, 512),))
    out_grad = noise(streams_of[1], (ROWS, OUT), 1.0, 6.0, ((0, 512),))
    route_keys = jax.random.split(jax.random.fold_in(streams_of[2], 1), ROWS // ROWS_DEV)
    route_turns = jax.random.permutation(jax.random.fold_in(streams_of[2], 3), ROWS // ROWS_DEV)
    route = jax.vmap(lambda own, number: shared_out(jax.random.fold_in(streams_of[2], 2), own, number, ROWS_DEV, EXPERTS, 1, CAP, 1))(route_keys, route_turns).reshape((ROWS, 1))
    coef = noise(streams_of[3], (GROUPS, IN, NB, COLS), (IN * NB) ** -0.5, 0.125, ((0, 128), (1, 4)))
    first_moment = noise(streams_of[4], (GROUPS, IN, NB, COLS), 3.0, 15.0, ((0, 128), (1, 4)))
    second_moment = jnp.clip(jnp.exp(math.log(100.0) - 4.6051702 * jax.random.uniform(streams_of[5], (GROUPS, IN, NB, COLS), jnp.float32) ** block_levels(streams_of[5], (GROUPS, IN, NB, COLS), ((0, 128), (1, 4)), -0.2, 0.2)), 1.0, 100.0).astype(jnp.bfloat16)
    return {"inputs": inputs, "out_grad": out_grad, "route": route, "coef": coef, "first_moment": first_moment, "second_moment": second_moment}


GRID_LOWER = -2.0
GRID_UPPER = 2.0
PENALTY = 10.0
LEARN_RATE = 0.001
BETA_ONE = 0.9
BETA_TWO = 0.999
EPSILON = 1e-08
WEIGHT_DECAY = 0.1
BIAS_ONE = 0.999973438601112
BIAS_TWO = 0.0952078528855534

def spline_bases(values):
    spacing = (GRID_UPPER - GRID_LOWER) / (NB - 3)
    offset = (values - (GRID_LOWER - 3.0 * spacing)) / spacing
    shifted = offset[..., None] - jnp.arange(NB, dtype=jnp.float32)
    inside = shifted < 4.0
    part_zero = jnp.maximum(shifted, 0.0)
    part_one = jnp.maximum(shifted - 1.0, 0.0)
    part_two = jnp.maximum(shifted - 2.0, 0.0)
    part_three = jnp.maximum(shifted - 3.0, 0.0)
    basis_value = (part_zero ** 3 - 4.0 * part_one ** 3 + 6.0 * part_two ** 3 - 4.0 * part_three ** 3) / 6.0
    slope_value = (part_zero * part_zero - 4.0 * part_one * part_one + 6.0 * part_two * part_two - 4.0 * part_three * part_three) * (0.5 / spacing)
    return (jnp.where(inside, basis_value, 0.0), jnp.where(inside, slope_value, 0.0))

def smooth_penalty(values):
    curvature = values[..., :-2, :] - 2.0 * values[..., 1:-1, :] + values[..., 2:, :]
    padding = [(0, 0)] * (values.ndim - 2) + [(2, 2), (0, 0)]
    padded = jnp.pad(curvature, padding)
    return padded[..., :-2, :] - 2.0 * padded[..., 1:-1, :] + padded[..., 2:, :]

def reference(inputs, out_grad, route, coef, first_moment, second_moment):
    total_rows = inputs.shape[0]
    expert_of = route[:, 0]
    order = jnp.argsort(expert_of, stable=True).astype(jnp.int32)
    counts = lax.optimization_barrier(jnp.sum((expert_of[:, None] == jnp.arange(EXPERTS, dtype=jnp.int32)[None, :]).astype(jnp.int32), axis=0))
    starts = (jnp.cumsum(counts) - counts).astype(jnp.int32)
    most_rows = N_EXPERT * N_DP * CAP
    padded_order = jnp.concatenate([order, jnp.zeros((most_rows,), jnp.int32)])

    def one_expert(expert_index):
        picked = lax.dynamic_slice_in_dim(padded_order, starts[expert_index], most_rows, 0)
        valid = jnp.arange(most_rows, dtype=jnp.int32) < counts[expert_index]
        chosen_inputs = inputs[picked]
        chosen_grads = jnp.where(valid[:, None], out_grad[picked], jnp.zeros((), jnp.bfloat16))
        values, slopes = spline_bases(chosen_inputs.astype(jnp.float32))
        basis_flat = values.astype(jnp.bfloat16).reshape(most_rows, IN * NB)
        weights = lax.dynamic_slice_in_dim(coef, expert_index * SPLIT, SPLIT, 0)
        grads_split = chosen_grads.reshape(most_rows, SPLIT, COLS)
        grad_parts = []
        partial_sum = jnp.zeros((most_rows, IN), jnp.float32)
        for column_group in range(SPLIT):
            block_grads = grads_split[:, column_group]
            grad_block = jnp.dot(basis_flat.T, block_grads, preferred_element_type=jnp.float32)
            weight_flat = weights[column_group].reshape(IN * NB, COLS)
            projected = jnp.dot(block_grads, weight_flat.T, preferred_element_type=jnp.float32)
            projected = projected.reshape(most_rows, IN, NB)
            partial_value = lax.optimization_barrier(jnp.sum(projected * slopes, axis=2)).astype(jnp.bfloat16)
            partial_sum = partial_sum + partial_value.astype(jnp.float32)
            grad_parts.append(grad_block.reshape(IN, NB, COLS))
        targets = jnp.where(valid, picked, total_rows).astype(jnp.int32)
        return (jnp.stack(grad_parts), partial_sum.astype(jnp.bfloat16), targets)
    grads, input_parts, targets = lax.map(one_expert, jnp.arange(EXPERTS, dtype=jnp.int32))
    input_grad = jnp.zeros((total_rows + 1, IN), jnp.bfloat16)
    input_grad = input_grad.at[targets.reshape(-1)].set(input_parts.reshape(-1, IN))[:total_rows]
    grad_all = grads.reshape(GROUPS, IN, NB, COLS)
    coef_float = coef.astype(jnp.float32)
    gradient = grad_all + PENALTY * smooth_penalty(coef_float)
    moment_one = BETA_ONE * first_moment.astype(jnp.float32) + (1.0 - BETA_ONE) * gradient
    moment_two = BETA_TWO * second_moment.astype(jnp.float32) + (1.0 - BETA_TWO) * gradient * gradient
    update = moment_one / BIAS_ONE / (jnp.sqrt(moment_two / BIAS_TWO) + EPSILON)
    new_coef = coef_float - LEARN_RATE * (update + WEIGHT_DECAY * coef_float)
    return (input_grad, new_coef.astype(jnp.bfloat16), moment_one.astype(jnp.bfloat16), moment_two.astype(jnp.bfloat16))
```

```python
import functools

import jax
import jax.numpy as jnp
from jax import lax
from jax.experimental import pallas as pl
from jax.experimental.pallas import tpu as pltpu
from jax.sharding import PartitionSpec as P

IN = 256
NB = 8
SPLIT = 4
COLS = 512
CAP = 8
ROWS = 128
LANES = 128
WIDTH = COLS + IN

PENALTY = 10.0
LEARN_RATE = 0.001
BETA_ONE = 0.9
BETA_TWO = 0.999
EPSILON = 1e-08
WEIGHT_DECAY = 0.1
BIAS_ONE = 0.999973438601112
BIAS_TWO = 0.0952078528855534
HALF_INV_SPACING = 0.625

f32 = jnp.float32
bf16 = jnp.bfloat16


def vmem(n):
    return [pl.BlockSpec(memory_space=pltpu.VMEM) for _ in range(n)]


def slot_matrix(route_row, slots):
    wide = jnp.broadcast_to(route_row.astype(f32), (ROWS, ROWS))
    tall = jnp.transpose(wide)
    earlier = lax.broadcasted_iota(jnp.int32, (ROWS, ROWS), 0) < lax.broadcasted_iota(
        jnp.int32, (ROWS, ROWS), 1
    )
    rank = jnp.sum(jnp.where((wide == tall) & earlier, 1.0, 0.0), axis=0, keepdims=True)
    slot = route_row * CAP + rank.astype(jnp.int32)
    hit = lax.broadcasted_iota(jnp.int32, (slots, ROWS), 0) == slot
    return jnp.where(hit, 1.0, 0.0).astype(bf16)


def dispatch_kernel(route_ref, inputs_ref, grads_ref, send_ref, onehot_ref):
    experts = send_ref.shape[0]
    onehot = slot_matrix(route_ref[...], experts * CAP)
    onehot_ref[...] = onehot
    sent = jnp.dot(onehot, inputs_ref[...], preferred_element_type=f32).astype(bf16)
    sent = sent.reshape(experts, CAP, IN)
    for s in range(SPLIT):
        block = jnp.dot(
            onehot, grads_ref[:, s * COLS : (s + 1) * COLS], preferred_element_type=f32
        ).astype(bf16)
        send_ref[:, s, :, 0:COLS] = block.reshape(experts, CAP, COLS)
        send_ref[:, s, :, COLS:WIDTH] = sent


def dispatch(route_row, inputs, out_grad, experts):
    return pl.pallas_call(
        dispatch_kernel,
        out_shape=(
            jax.ShapeDtypeStruct((experts, SPLIT, CAP, WIDTH), bf16),
            jax.ShapeDtypeStruct((experts * CAP, ROWS), bf16),
        ),
        in_specs=vmem(3),
        out_specs=tuple(vmem(2)),
        name="dispatch",
    )(route_row, inputs, out_grad)


def relayout_kernel(coef_ref, out_ref, wide_ref):
    quarter = out_ref.shape[1]
    for j in range(COLS // LANES):
        at = slice(j * LANES, (j + 1) * LANES)
        wide_ref[j] = coef_ref[:, :, at].reshape(quarter * NB, LANES).astype(f32)
        for k in range(NB):
            out_ref[k, :, at] = wide_ref[j, pl.ds(k, quarter, stride=NB), :].astype(bf16)


def relayout(coef):
    quarter = coef.shape[0]
    return pl.pallas_call(
        relayout_kernel,
        out_shape=jax.ShapeDtypeStruct((NB, quarter, COLS), bf16),
        in_specs=vmem(1),
        out_specs=vmem(1)[0],
        scratch_shapes=[pltpu.VMEM((COLS // LANES, quarter * NB, LANES), f32)],
        name="relayout",
    )(coef)


def cells(x):
    t = x.astype(f32) * 1.25 + 5.5
    cell = jnp.floor(t)
    return cell, t - cell


def pick(cell, k, pieces):
    out = jnp.where(cell == float(k + 3), pieces[3], 0.0)
    for j in (2, 1, 0):
        out = jnp.where(cell == float(k + j), pieces[j], out)
    return out


def project_kernel(data_ref, coef_ref, partial_ref, turned_ref):
    x = data_ref[:, COLS:WIDTH]
    cell, f = cells(x)
    g = 1.0 - f
    c = HALF_INV_SPACING
    pieces = (
        c * f * f,
        c + f * (2.0 * c - 3.0 * c * f),
        -c - g * (2.0 * c - 3.0 * c * g),
        -c * g * g,
    )
    grads = data_ref[:, 0:COLS]
    total = None
    for k in range(NB):
        projected = lax.dot_general(
            grads, coef_ref[k], (((1,), (1,)), ((), ())), preferred_element_type=f32
        )
        term = projected * pick(cell, k, pieces)
        total = term if total is None else total + term
    partial_ref[...] = total.astype(bf16)
    turned_ref[...] = jnp.transpose(x.astype(f32)).astype(bf16)


def project(data, coef_all):
    slots = data.shape[0]
    step = 256
    return pl.pallas_call(
        project_kernel,
        grid=(slots // step,),
        out_shape=(
            jax.ShapeDtypeStruct((slots, IN), bf16),
            jax.ShapeDtypeStruct((IN, slots), bf16),
        ),
        in_specs=[
            pl.BlockSpec((step, WIDTH), lambda i: (i, 0)),
            pl.BlockSpec((NB, IN, COLS), lambda i: (0, 0, 0)),
        ],
        out_specs=(
            pl.BlockSpec((step, IN), lambda i: (i, 0)),
            pl.BlockSpec((IN, step), lambda i: (0, i)),
        ),
        name="project",
    )(data, coef_all)


def gradient_kernel(first_ref, turned_ref, data_ref, *refs):
    outs, basis_ref = refs[:-1], refs[-1]
    quarter = turned_ref.shape[0] // len(outs)
    for turn, out_ref in enumerate(outs):
        start = lax.rem(first_ref[0] + turn, len(outs)) * quarter
        x = turned_ref[pl.ds(pl.multiple_of(start, quarter), quarter), :]
        cell, f = cells(x)
        g = 1.0 - f
        c = 1.0 / 6.0
        pieces = (
            c * f * f * f,
            c + f * (0.5 + f * (0.5 - 0.5 * f)),
            c + g * (0.5 + g * (0.5 - 0.5 * g)),
            c * g * g * g,
        )
        for k in range(NB):
            basis_ref[turn % 2, k * quarter : (k + 1) * quarter, :] = pick(cell, k, pieces).astype(bf16)
        out_ref[...] = (
            jnp.dot(basis_ref[turn % 2], data_ref[...], preferred_element_type=f32)
            .astype(bf16)
            .reshape(out_ref.shape)
        )


def gradient(first, turned, data, members):
    quarter = IN // members
    slots = data.shape[0]
    return pl.pallas_call(
        gradient_kernel,
        grid=(1,),
        out_shape=tuple(jax.ShapeDtypeStruct((NB, quarter, COLS), bf16) for _ in range(members)),
        in_specs=[
            pl.BlockSpec(memory_space=pltpu.SMEM),
            pl.BlockSpec((IN, slots), lambda i: (0, 0)),
            pl.BlockSpec((slots, COLS), lambda i: (0, 0)),
        ],
        out_specs=tuple(pl.BlockSpec((NB, quarter, COLS), lambda i: (0, 0, 0)) for _ in range(members)),
        scratch_shapes=[pltpu.VMEM((2, NB * quarter, slots), bf16)],
        name="gradient",
    )(first, turned, data)


def adam_kernel(*refs):
    parts = refs[: len(refs) - 7]
    coef_ref, one_ref, two_ref, new_ref, one_out, two_out, wide_ref = refs[len(refs) - 7 :]
    rows = coef_ref.shape[0]
    for k in range(NB):
        piece = parts[0][k].astype(f32)
        for part in parts[1:]:
            piece = piece + part[k].astype(f32)
        for j in range(COLS // LANES):
            wide_ref[j, pl.ds(k, rows, stride=NB), :] = piece[:, j * LANES : (j + 1) * LANES]
    grad = jnp.concatenate(
        [wide_ref[j].reshape(rows, NB, LANES) for j in range(COLS // LANES)], axis=2
    )
    c = coef_ref[...].astype(f32)
    k = lax.broadcasted_iota(jnp.int32, (1, NB, COLS), 1)

    def row(values):
        out = jnp.full((1, NB, COLS), float(values[0]), f32)
        for index in range(1, NB):
            if values[index] != values[0]:
                out = jnp.where(k == index, float(values[index]), out)
        return out

    pen = c * row((1, 5, 6, 6, 6, 6, 5, 1))
    pen = pen + pltpu.roll(c, 1, 1) * row((0, -2, -4, -4, -4, -4, -4, -2))
    pen = pen + pltpu.roll(c, NB - 1, 1) * row((-2, -4, -4, -4, -4, -4, -2, 0))
    pen = pen + pltpu.roll(c, 2, 1) * row((0, 0, 1, 1, 1, 1, 1, 1))
    pen = pen + pltpu.roll(c, NB - 2, 1) * row((1, 1, 1, 1, 1, 1, 0, 0))
    gradient_all = grad + PENALTY * pen
    one = BETA_ONE * one_ref[...].astype(f32) + (1.0 - BETA_ONE) * gradient_all
    two = BETA_TWO * two_ref[...].astype(f32) + (1.0 - BETA_TWO) * gradient_all * gradient_all
    update = one * (1.0 / BIAS_ONE) / (jnp.sqrt(two * (1.0 / BIAS_TWO)) + EPSILON)
    new_ref[...] = (c - LEARN_RATE * (update + WEIGHT_DECAY * c)).astype(bf16)
    one_out[...] = one.astype(bf16)
    two_out[...] = two.astype(bf16)


def adam(parts, coef, one, two):
    quarter = coef.shape[0]
    step = 16
    major = pl.BlockSpec((NB, step, COLS), lambda i: (0, i, 0))
    state = pl.BlockSpec((step, NB, COLS), lambda i: (i, 0, 0))
    return pl.pallas_call(
        adam_kernel,
        grid=(quarter // step,),
        out_shape=tuple(jax.ShapeDtypeStruct(coef.shape, bf16) for _ in range(3)),
        in_specs=[major] * len(parts) + [state] * 3,
        out_specs=(state,) * 3,
        scratch_shapes=[pltpu.VMEM((COLS // LANES, step * NB, LANES), f32)],
        name="adam",
    )(*parts, coef, one, two)


def combine_kernel(returned_ref, onehot_ref, out_ref):
    experts = returned_ref.shape[0]
    total = returned_ref[:, 0].astype(f32)
    for s in range(1, SPLIT):
        total = total + returned_ref[:, s].astype(f32)
    total = total.astype(bf16).reshape(experts * CAP, IN)
    out_ref[...] = lax.dot_general(
        onehot_ref[...], total, (((0,), (0,)), ((), ())), preferred_element_type=f32
    ).astype(bf16)


def combine(returned, onehot):
    return pl.pallas_call(
        combine_kernel,
        out_shape=jax.ShapeDtypeStruct((ROWS, IN), bf16),
        in_specs=vmem(2),
        out_specs=vmem(1)[0],
        name="combine",
    )(returned, onehot)


def on_device(inputs, out_grad, route, coef, first_moment, second_moment):
    groups = lax.axis_size("expert")
    members = lax.axis_size("dp")
    experts = groups // SPLIT
    here = lax.axis_index("dp")
    quarter = IN // members

    def shift(value, by):
        return lax.ppermute(value, "dp", [(i, (i + by) % members) for i in range(members)])

    send, onehot = dispatch(route.reshape(1, ROWS), inputs, out_grad, experts)
    got = lax.all_to_all(
        send.reshape(groups, CAP, WIDTH), "expert", split_axis=0, concat_axis=0, tiled=True
    ).reshape(groups * CAP, WIDTH)

    own = relayout(coef[0])
    coef_all = jnp.zeros((NB, IN, COLS), bf16)
    for turn in range(members):
        piece = own if turn == 0 else shift(own, -turn)
        at = lax.rem(here + turn, members) * quarter
        coef_all = lax.dynamic_update_slice(coef_all, piece, (0, at, 0))

    partial, turned = project(got, coef_all)
    returned = lax.all_to_all(
        partial.reshape(groups, CAP, IN), "expert", split_axis=0, concat_axis=0, tiled=True
    )
    pieces = gradient(here.reshape(1), turned, got, members)
    parts = [pieces[0]] + [shift(pieces[turn], turn) for turn in range(1, members)]
    new_coef, new_one, new_two = adam(parts, coef[0], first_moment[0], second_moment[0])
    input_grad = combine(returned.reshape(experts, SPLIT, CAP, IN), onehot)
    return input_grad, new_coef[None], new_one[None], new_two[None]


def solution(mesh):
    rows = P(("expert", "dp"), None)
    state = P("expert", "dp", None, None)
    return jax.shard_map(
        on_device,
        mesh=mesh,
        in_specs=(rows, rows, rows, state, state, state),
        out_specs=(rows, state, state, state),
        check_vma=False,
    )
```

```python
import functools

import jax
import jax.numpy as jnp
from jax import lax
from jax.experimental import pallas as pl
from jax.experimental.pallas import tpu as pltpu
from jax.sharding import PartitionSpec as P

IN = 256
NB = 8
SPLIT = 4
COLS = 512
CAP = 8
ROWS = 128
LANES = 128
WIDTH = COLS + IN

PENALTY = 10.0
LEARN_RATE = 0.001
BETA_ONE = 0.9
BETA_TWO = 0.999
EPSILON = 1e-08
WEIGHT_DECAY = 0.1
BIAS_ONE = 0.999973438601112
BIAS_TWO = 0.0952078528855534
HALF_INV_SPACING = 0.625

f32 = jnp.float32
bf16 = jnp.bfloat16


LIMIT = pltpu.CompilerParams(vmem_limit_bytes=28 * 1024 * 1024)


SCALARS = pl.BlockSpec(memory_space=pltpu.SMEM)


ANYWHERE = pl.BlockSpec(memory_space=pl.ANY)


TOKEN = jax.ShapeDtypeStruct((8, LANES), jnp.float32)


def vmem(n):
    return [pl.BlockSpec(memory_space=pltpu.VMEM) for _ in range(n)]


def slot_matrix(route_row, slots):
    wide = jnp.broadcast_to(route_row.astype(f32), (ROWS, ROWS))
    tall = jnp.transpose(wide)
    earlier = lax.broadcasted_iota(jnp.int32, (ROWS, ROWS), 0) < lax.broadcasted_iota(
        jnp.int32, (ROWS, ROWS), 1
    )
    rank = jnp.sum(jnp.where((wide == tall) & earlier, 1.0, 0.0), axis=0, keepdims=True)
    slot = route_row * CAP + rank.astype(jnp.int32)
    hit = lax.broadcasted_iota(jnp.int32, (slots, ROWS), 0) == slot
    return jnp.where(hit, 1.0, 0.0).astype(bf16)


def dispatch_kernel(route_ref, inputs_ref, grads_ref, send_ref, onehot_ref):
    experts = send_ref.shape[0]
    onehot = slot_matrix(route_ref[...], experts * CAP)
    onehot_ref[...] = onehot
    sent = jnp.dot(onehot, inputs_ref[...], preferred_element_type=f32).astype(bf16)
    sent = sent.reshape(experts, CAP, IN)
    for s in range(SPLIT):
        block = jnp.dot(
            onehot, grads_ref[:, s * COLS : (s + 1) * COLS], preferred_element_type=f32
        ).astype(bf16)
        send_ref[:, s, :, 0:COLS] = block.reshape(experts, CAP, COLS)
        send_ref[:, s, :, COLS:WIDTH] = sent


def dispatch(route_row, inputs, out_grad, experts):
    return pl.pallas_call(
        dispatch_kernel,
        out_shape=(
            jax.ShapeDtypeStruct((experts, SPLIT, CAP, WIDTH), bf16),
            jax.ShapeDtypeStruct((experts * CAP, ROWS), bf16),
        ),
        in_specs=vmem(3),
        out_specs=tuple(vmem(2)),
        name="dispatch",
    )(route_row, inputs, out_grad)


def prepare_kernel(coef_ref, out_ref, pen_ref, wide_ref):
    quarter = out_ref.shape[1]
    for j in range(COLS // LANES):
        at = slice(j * LANES, (j + 1) * LANES)
        wide_ref[j] = coef_ref[:, :, at].reshape(quarter * NB, LANES).astype(f32)
        for k in range(NB):
            out_ref[k, :, at] = wide_ref[j, pl.ds(k, quarter, stride=NB), :].astype(bf16)
    k = lax.broadcasted_iota(jnp.int32, (1, NB, COLS), 1)

    def row(values):
        out = jnp.full((1, NB, COLS), float(values[0]), f32)
        for index in range(1, NB):
            if values[index] != values[0]:
                out = jnp.where(k == index, float(values[index]), out)
        return out * PENALTY

    rows = (
        row((1, 5, 6, 6, 6, 6, 5, 1)),
        row((0, -2, -4, -4, -4, -4, -4, -2)),
        row((0, 0, 1, 1, 1, 1, 1, 1)),
        row((1, 1, 1, 1, 1, 1, 0, 0)),
        row((-2, -4, -4, -4, -4, -4, -2, 0)),
    )
    for i in range(0, quarter, 4):
        c = coef_ref[i : i + 4].astype(f32)
        pen = c * rows[0]
        for turn, weight in zip((1, 2, NB - 2, NB - 1), rows[1:]):
            pen = pen + pltpu.roll(c, turn, 1) * weight
        pen_ref[i : i + 4] = pen


def prepare(coef):
    quarter = coef.shape[0]
    return pl.pallas_call(
        prepare_kernel,
        out_shape=(
            jax.ShapeDtypeStruct((NB, quarter, COLS), bf16),
            jax.ShapeDtypeStruct((quarter, NB, COLS), f32),
        ),
        in_specs=vmem(1),
        out_specs=tuple(vmem(2)),
        scratch_shapes=[pltpu.VMEM((COLS // LANES, quarter * NB, LANES), f32)],
        compiler_params=LIMIT,
        name="prepare",
    )(coef)


def cells(x):
    t = x.astype(f32) * 1.25 + 5.5
    cell = jnp.floor(t)
    return cell, t - cell


def turned_pieces(cell, pieces):
    whole = cell.astype(jnp.int32)
    odd = (whole & 1) == 1
    high = (whole & 2) == 2
    s0, s1, s2, s3 = pieces
    a = (
        jnp.where(odd, s1, s0),
        jnp.where(odd, s0, s3),
        jnp.where(odd, s3, s2),
        jnp.where(odd, s2, s1),
    )
    v = [jnp.where(high, a[q - 2], a[q]) for q in range(4)]
    v[0] = jnp.where(cell < 8.0, v[0], 0.0)
    v[1] = jnp.where((cell >= 1.0) & (cell < 9.0), v[1], 0.0)
    v[2] = jnp.where((cell >= 2.0) & (cell < 10.0), v[2], 0.0)
    v[3] = jnp.where(cell >= 3.0, v[3], 0.0)
    return v


def assemble_kernel(place_ref, own_ref, first_ref, pair_ref, out_ref, done_ref):
    done_ref[...] = jnp.zeros_like(done_ref)
    out_ref[place_ref[0]] = own_ref[...]
    out_ref[place_ref[1]] = first_ref[...]
    out_ref[place_ref[2]] = pair_ref[0]
    out_ref[place_ref[3]] = pair_ref[1]


def assemble(place, own, first, pair):
    return pl.pallas_call(
        assemble_kernel,
        out_shape=(jax.ShapeDtypeStruct((4,) + own.shape, bf16), TOKEN),
        in_specs=[SCALARS] + vmem(3),
        out_specs=tuple(vmem(2)),
        compiler_params=LIMIT,
        name="assemble",
    )(place, own, first, pair)


def project_kernel(data_ref, coef_ref, after_ref, out_ref, done_ref, wide_ref, partial_ref, sems):
    done_ref[...] = jnp.zeros_like(done_ref)
    copies = []
    slots = data_ref.shape[0]
    step = wide_ref.shape[2]
    small = 32
    c = HALF_INV_SPACING
    for block in range(slots // step):
        at = slice(block * step, (block + 1) * step)
        for k in range(NB):
            weight = jnp.concatenate([coef_ref[q, k] for q in range(coef_ref.shape[0])], axis=0)
            wide_ref[block % 2, k] = lax.dot_general(
                data_ref[at, 0:COLS], weight, (((1,), (1,)), ((), ())), preferred_element_type=f32
            )
        for low in range(0, step, small):
            here = slice(low, low + small)
            rows = slice(block * step + low, block * step + low + small)
            cell, f = cells(data_ref[rows, COLS:WIDTH])
            g = 1.0 - f
            v = turned_pieces(
                cell,
                (
                    c * f * f,
                    c + f * (2.0 * c - 3.0 * c * f),
                    -c - g * (2.0 * c - 3.0 * c * g),
                    -c * g * g,
                ),
            )
            total = None
            for q in range(4):
                live = jnp.where(
                    cell < float(q + 4), wide_ref[block % 2, q, here], wide_ref[block % 2, q + 4, here]
                )
                term = v[q] * live
                total = term if total is None else total + term
            partial_ref[rows, :] = total.astype(bf16)
        copies.append(pltpu.make_async_copy(partial_ref.at[at], out_ref.at[at], sems.at[block]))
        copies[-1].start()
    for copy in copies:
        copy.wait()


def project(data, coefs, after):
    slots = data.shape[0]
    step = 256
    return pl.pallas_call(
        project_kernel,
        out_shape=(pltpu.HBM((slots, IN), bf16), TOKEN),
        in_specs=vmem(2) + [ANYWHERE],
        out_specs=(pl.BlockSpec(memory_space=pltpu.HBM), vmem(1)[0]),
        scratch_shapes=[
            pltpu.VMEM((2, NB, step, IN), f32),
            pltpu.VMEM((slots, IN), bf16),
            pltpu.SemaphoreType.DMA((slots // step,)),
        ],
        compiler_params=LIMIT,
        cost_estimate=pl.CostEstimate(flops=2200000000, bytes_accessed=8000000, transcendentals=0),
        name="project",
    )(data, coefs, after)


def fill_basis(basis_ref, x_ref, start, quarter):
    slots = x_ref.shape[1]
    c = 1.0 / 6.0
    high, wide = 16, 256
    for low in range(0, quarter, high):
        for left in range(0, slots, wide):
            rows = pl.ds(pl.multiple_of(start + low, high), high)
            cell, f = cells(x_ref[rows, left : left + wide])
            g = 1.0 - f
            v = turned_pieces(
                cell,
                (
                    c * f * f * f,
                    c + f * (0.5 + f * (0.5 - 0.5 * f)),
                    c + g * (0.5 + g * (0.5 - 0.5 * g)),
                    c * g * g * g,
                ),
            )
            for q in range(4):
                below = cell < float(q + 4)
                for k, value in (
                    (q, jnp.where(below, v[q], 0.0)),
                    (q + 4, jnp.where(below, 0.0, v[q])),
                ):
                    at = k * quarter + low
                    basis_ref[at : at + high, left : left + wide] = value.astype(bf16)


def bases_dot(basis_ref, turned_ref, data_ref, start, quarter):
    fill_basis(basis_ref, turned_ref, start, quarter)
    return jnp.dot(basis_ref[...], data_ref[:, 0:COLS], preferred_element_type=f32).reshape(
        NB, quarter, COLS
    )


def pair_kernel(place_ref, data_ref, after_ref, out_ref, turned_ref, done_ref, basis_ref):
    done_ref[...] = jnp.zeros_like(done_ref)
    same = lax.broadcasted_iota(jnp.int32, (IN, IN), 0) == lax.broadcasted_iota(
        jnp.int32, (IN, IN), 1
    )
    turned_ref[...] = lax.dot_general(
        jnp.where(same, 1.0, 0.0).astype(bf16),
        data_ref[:, COLS:WIDTH],
        (((1,), (1,)), ((), ())),
        preferred_element_type=f32,
    ).astype(bf16)
    quarter = out_ref.shape[2]
    for index, which in enumerate((1, 3)):
        out_ref[index] = bases_dot(
            basis_ref.at[index], turned_ref, data_ref, place_ref[which] * quarter, quarter
        ).astype(bf16)


def pair(place, data, after, quarter):
    slots = data.shape[0]
    return pl.pallas_call(
        pair_kernel,
        out_shape=(
            jax.ShapeDtypeStruct((2, NB, quarter, COLS), bf16),
            jax.ShapeDtypeStruct((IN, slots), bf16),
            TOKEN,
        ),
        in_specs=[SCALARS] + vmem(1) + [ANYWHERE],
        out_specs=tuple(vmem(3)),
        scratch_shapes=[pltpu.VMEM((2, NB * quarter, slots), bf16)],
        compiler_params=LIMIT,
        cost_estimate=pl.CostEstimate(flops=1100000000, bytes_accessed=4000000, transcendentals=0),
        name="pair",
    )(place, data, after)


def last_kernel(place_ref, turned_ref, data_ref, came_ref, after_ref, out_ref, done_ref, basis_ref):
    done_ref[...] = jnp.zeros_like(done_ref)
    quarter = out_ref.shape[1]
    piece = bases_dot(basis_ref, turned_ref, data_ref, place_ref[2] * quarter, quarter)
    out_ref[...] = (piece + came_ref[1].astype(f32)).astype(bf16)


def last_piece(place, turned, data, came, after, quarter):
    slots = data.shape[0]
    return pl.pallas_call(
        last_kernel,
        out_shape=(jax.ShapeDtypeStruct((NB, quarter, COLS), bf16), TOKEN),
        in_specs=[SCALARS] + vmem(3) + [ANYWHERE],
        out_specs=tuple(vmem(2)),
        scratch_shapes=[pltpu.VMEM((NB * quarter, slots), bf16)],
        compiler_params=LIMIT,
        name="last_piece",
    )(place, turned, data, came, after)


def own_kernel(
    place_ref, turned_ref, data_ref, came_ref, pen_ref, after_ref, out_ref, basis_ref, wide_ref
):
    quarter = out_ref.shape[0]
    piece = bases_dot(basis_ref, turned_ref, data_ref, place_ref[0] * quarter, quarter)
    piece = piece + came_ref[0].astype(f32)
    for j in range(COLS // LANES):
        lanes = slice(j * LANES, (j + 1) * LANES)
        for k in range(NB):
            wide_ref[j, pl.ds(k, quarter, stride=NB), :] = piece[k, :, lanes]
        out_ref[:, :, lanes] = wide_ref[j].reshape(quarter, NB, LANES) + pen_ref[:, :, lanes]


def own_piece(place, turned, data, came, pen, after):
    slots = data.shape[0]
    quarter = pen.shape[0]
    return pl.pallas_call(
        own_kernel,
        out_shape=jax.ShapeDtypeStruct(pen.shape, f32),
        in_specs=[SCALARS] + vmem(4) + [ANYWHERE],
        out_specs=vmem(1)[0],
        scratch_shapes=[
            pltpu.VMEM((NB * quarter, slots), bf16),
            pltpu.VMEM((COLS // LANES, NB * quarter, LANES), f32),
        ],
        compiler_params=LIMIT,
        name="own_piece",
    )(place, turned, data, came, pen, after)


def adam_kernel(
    last_ref, sum_ref, coef_ref, one_ref, two_ref, new_ref, one_out, two_out, done_ref, wide_ref
):
    done_ref[...] = jnp.zeros_like(done_ref)
    rows = coef_ref.shape[0]
    small = 4
    for j in range(COLS // LANES):
        lanes = slice(j * LANES, (j + 1) * LANES)
        for k in range(NB):
            wide_ref[j, pl.ds(k, rows, stride=NB), :] = last_ref[k, :, lanes].astype(f32)
    for low in range(0, rows, small):
        at = slice(low, low + small)
        grad = jnp.concatenate(
            [
                wide_ref[j, low * NB : (low + small) * NB].reshape(small, NB, LANES)
                for j in range(COLS // LANES)
            ],
            axis=2,
        )
        grad = grad + sum_ref[at]
        c = coef_ref[at].astype(f32)
        one = BETA_ONE * one_ref[at].astype(f32) + (1.0 - BETA_ONE) * grad
        two = BETA_TWO * two_ref[at].astype(f32) + (1.0 - BETA_TWO) * grad * grad
        scaled = two * (1.0 / BIAS_TWO)
        root = scaled * lax.rsqrt(scaled)
        update = one * (1.0 / BIAS_ONE) / (root + EPSILON)
        new_ref[at] = (c - LEARN_RATE * (update + WEIGHT_DECAY * c)).astype(bf16)
        one_out[at] = one.astype(bf16)
        two_out[at] = two.astype(bf16)


def adam(last, total, coef, one, two):
    quarter = coef.shape[0]
    return pl.pallas_call(
        adam_kernel,
        out_shape=tuple(jax.ShapeDtypeStruct(coef.shape, bf16) for _ in range(3)) + (TOKEN,),
        in_specs=vmem(5),
        out_specs=tuple(vmem(4)),
        scratch_shapes=[pltpu.VMEM((COLS // LANES, quarter * NB, LANES), f32)],
        compiler_params=LIMIT,
        name="adam",
    )(last, total, coef, one, two)


def combine_kernel(returned_ref, onehot_ref, after_ref, out_ref):
    experts = returned_ref.shape[0]
    total = returned_ref[:, 0].astype(f32)
    for s in range(1, SPLIT):
        total = total + returned_ref[:, s].astype(f32)
    total = total.astype(bf16).reshape(experts * CAP, IN)
    out_ref[...] = lax.dot_general(
        onehot_ref[...], total, (((0,), (0,)), ((), ())), preferred_element_type=f32
    ).astype(bf16)


def combine(returned, onehot, after):
    return pl.pallas_call(
        combine_kernel,
        out_shape=jax.ShapeDtypeStruct((ROWS, IN), bf16),
        in_specs=vmem(2) + [ANYWHERE],
        out_specs=vmem(1)[0],
        compiler_params=LIMIT,
        name="combine",
    )(returned, onehot, after)


def on_device(inputs, out_grad, route, coef, first_moment, second_moment):
    groups = lax.axis_size("expert")
    members = lax.axis_size("dp")
    experts = groups // SPLIT
    quarter = IN // members
    core = lax.axis_index("expert") % 2
    here = lax.axis_index("dp")
    place = jnp.stack([here, here ^ (1 + 2 * core), here ^ (3 - 2 * core), here ^ 2])

    def swap(value, masks):
        pairs = [
            (g * members + (m ^ masks[g % 2]), g * members + m)
            for g in range(groups)
            for m in range(members)
        ]
        return lax.ppermute(value, ("expert", "dp"), pairs)

    send, onehot = dispatch(route.reshape(1, ROWS), inputs, out_grad, experts)
    got = lax.all_to_all(
        send.reshape(groups, CAP, WIDTH), "expert", split_axis=0, concat_axis=0, tiled=True
    ).reshape(groups * CAP, WIDTH)

    own, pen = prepare(coef[0])
    first_coef = swap(own, (1, 3))
    coefs, done = assemble(place, own, first_coef, swap(jnp.stack([own, first_coef]), (3, 1)))

    sent, turned, done = pair(place, got, done, quarter)
    came = swap(sent, (1, 3))
    partial, done = project(got, coefs, done)
    returned = lax.all_to_all(
        partial.reshape(groups, CAP, IN), "expert", split_axis=0, concat_axis=0, tiled=True
    )
    sent_last, done = last_piece(place, turned, got, came, done, quarter)
    last = swap(sent_last, (3, 1))
    total = own_piece(place, turned, got, came, pen, done)
    new_coef, new_one, new_two, done = adam(
        last, total, coef[0], first_moment[0], second_moment[0]
    )
    input_grad = combine(returned.reshape(experts, SPLIT, CAP, IN), onehot, done)
    return input_grad, new_coef[None], new_one[None], new_two[None]


def solution(mesh):
    rows = P(("expert", "dp"), None)
    state = P("expert", "dp", None, None)
    return jax.shard_map(
        on_device,
        mesh=mesh,
        in_specs=(rows, rows, rows, state, state, state),
        out_specs=(rows, state, state, state),
        check_vma=False,
    )
```

```python
import functools

import jax
import jax.numpy as jnp
from jax import lax
from jax.experimental import pallas as pl
from jax.experimental.pallas import tpu as pltpu
from jax.sharding import PartitionSpec as P

IN = 256
NB = 8
SPLIT = 4
COLS = 512
CAP = 8
ROWS = 128
LANES = 128
HALF = IN // 2
WIDTH = COLS + HALF

PENALTY = 10.0
LEARN_RATE = 0.001
BETA_ONE = 0.9
BETA_TWO = 0.999
EPSILON = 1e-08
WEIGHT_DECAY = 0.1
BIAS_ONE = 0.999973438601112
BIAS_TWO = 0.0952078528855534
HALF_INV_SPACING = 0.625

f32 = jnp.float32
bf16 = jnp.bfloat16


LIMIT = pltpu.CompilerParams(vmem_limit_bytes=28 * 1024 * 1024)


SCALARS = pl.BlockSpec(memory_space=pltpu.SMEM)


ANYWHERE = pl.BlockSpec(memory_space=pl.ANY)


TOKEN = jax.ShapeDtypeStruct((8, LANES), jnp.float32)


def vmem(n):
    return [pl.BlockSpec(memory_space=pltpu.VMEM) for _ in range(n)]


def slot_matrix(route_row, slots):
    wide = jnp.broadcast_to(route_row.astype(f32), (ROWS, ROWS))
    tall = jnp.transpose(wide)
    earlier = lax.broadcasted_iota(jnp.int32, (ROWS, ROWS), 0) < lax.broadcasted_iota(
        jnp.int32, (ROWS, ROWS), 1
    )
    rank = jnp.sum(jnp.where((wide == tall) & earlier, 1.0, 0.0), axis=0, keepdims=True)
    slot = route_row * CAP + rank.astype(jnp.int32)
    hit = lax.broadcasted_iota(jnp.int32, (slots, ROWS), 0) == slot
    return jnp.where(hit, 1.0, 0.0).astype(bf16)


def dispatch_kernel(route_ref, inputs_ref, grads_ref, send_ref, onehot_ref):
    experts = send_ref.shape[0]
    onehot = slot_matrix(route_ref[...], experts * CAP)
    onehot_ref[...] = onehot
    sent = jnp.dot(onehot, inputs_ref[...], preferred_element_type=f32).astype(bf16)
    sent = sent.reshape(experts, CAP, IN)
    for s in range(SPLIT):
        block = jnp.dot(
            onehot, grads_ref[:, s * COLS : (s + 1) * COLS], preferred_element_type=f32
        ).astype(bf16)
        send_ref[:, s, :, 0:COLS] = block.reshape(experts, CAP, COLS)
        send_ref[:, s, :, COLS:WIDTH] = sent[:, :, (s % 2) * HALF : (s % 2 + 1) * HALF]


def dispatch(route_row, inputs, out_grad, experts):
    return pl.pallas_call(
        dispatch_kernel,
        out_shape=(
            jax.ShapeDtypeStruct((experts, SPLIT, CAP, WIDTH), bf16),
            jax.ShapeDtypeStruct((experts * CAP, ROWS), bf16),
        ),
        in_specs=vmem(3),
        out_specs=tuple(vmem(2)),
        name="dispatch",
    )(route_row, inputs, out_grad)


def prepare_kernel(coef_ref, out_ref, wide_ref):
    quarter = out_ref.shape[1]
    for j in range(COLS // LANES):
        at = slice(j * LANES, (j + 1) * LANES)
        wide_ref[j] = coef_ref[:, :, at].reshape(quarter * NB, LANES).astype(f32)
        for k in range(NB):
            out_ref[k, :, at] = wide_ref[j, pl.ds(k, quarter, stride=NB), :].astype(bf16)


def prepare(coef):
    quarter = coef.shape[0]
    return pl.pallas_call(
        prepare_kernel,
        out_shape=jax.ShapeDtypeStruct((NB, quarter, COLS), bf16),
        in_specs=vmem(1),
        out_specs=vmem(1)[0],
        scratch_shapes=[pltpu.VMEM((COLS // LANES, quarter * NB, LANES), f32)],
        compiler_params=LIMIT,
        name="prepare",
    )(coef)


def penalty_rows():
    k = lax.broadcasted_iota(jnp.int32, (1, NB, COLS), 1)

    def row(values):
        out = jnp.full((1, NB, COLS), float(values[0]), f32)
        for index in range(1, NB):
            if values[index] != values[0]:
                out = jnp.where(k == index, float(values[index]), out)
        return out * PENALTY

    return (
        row((1, 5, 6, 6, 6, 6, 5, 1)),
        row((0, -2, -4, -4, -4, -4, -4, -2)),
        row((0, 0, 1, 1, 1, 1, 1, 1)),
        row((1, 1, 1, 1, 1, 1, 0, 0)),
        row((-2, -4, -4, -4, -4, -4, -2, 0)),
    )


def cells(x):
    t = x.astype(f32) * 1.25 + 5.5
    cell = jnp.floor(t)
    return cell, t - cell


def turned_pieces(cell, pieces):
    whole = cell.astype(jnp.int32)
    odd = (whole & 1) == 1
    high = (whole & 2) == 2
    s0, s1, s2, s3 = pieces
    a = (
        jnp.where(odd, s1, s0),
        jnp.where(odd, s0, s3),
        jnp.where(odd, s3, s2),
        jnp.where(odd, s2, s1),
    )
    v = [jnp.where(high, a[q - 2], a[q]) for q in range(4)]
    v[0] = jnp.where(cell < 8.0, v[0], 0.0)
    v[1] = jnp.where((cell >= 1.0) & (cell < 9.0), v[1], 0.0)
    v[2] = jnp.where((cell >= 2.0) & (cell < 10.0), v[2], 0.0)
    v[3] = jnp.where(cell >= 3.0, v[3], 0.0)
    return v


def assemble_kernel(place_ref, own_ref, first_ref, second_ref, third_ref, out_ref, done_ref):
    done_ref[...] = jnp.zeros_like(done_ref)
    out_ref[place_ref[0]] = own_ref[...]
    out_ref[place_ref[1]] = first_ref[...]
    out_ref[place_ref[2]] = second_ref[...]
    out_ref[place_ref[3]] = third_ref[...]


def assemble(place, own, first, second, third):
    return pl.pallas_call(
        assemble_kernel,
        out_shape=(jax.ShapeDtypeStruct((4,) + own.shape, bf16), TOKEN),
        in_specs=[SCALARS] + vmem(4),
        out_specs=tuple(vmem(2)),
        compiler_params=LIMIT,
        name="assemble",
    )(place, own, first, second, third)


def take_kernel(data_ref, after_ref, out_ref):
    out_ref[...] = data_ref[:, COLS:WIDTH]


def take(data, after):
    return pl.pallas_call(
        take_kernel,
        out_shape=jax.ShapeDtypeStruct((data.shape[0], HALF), bf16),
        in_specs=vmem(1) + [ANYWHERE],
        out_specs=vmem(1)[0],
        compiler_params=LIMIT,
        name="take",
    )(data, after)


def project_kernel(data_ref, x_ref, coef_ref, after_ref, out_ref, done_ref, wide_ref, partial_ref, sems):
    done_ref[...] = jnp.zeros_like(done_ref)
    copies = []
    slots = data_ref.shape[0]
    step = wide_ref.shape[2]
    small = 32
    c = HALF_INV_SPACING
    for block in range(slots // step):
        at = slice(block * step, (block + 1) * step)
        for k in range(NB):
            weight = jnp.concatenate([coef_ref[q, k] for q in range(coef_ref.shape[0])], axis=0)
            wide_ref[block % 2, k] = lax.dot_general(
                data_ref[at, 0:COLS], weight, (((1,), (1,)), ((), ())), preferred_element_type=f32
            )
        for low in range(0, step, small):
            here = slice(low, low + small)
            rows = slice(block * step + low, block * step + low + small)
            cell, f = cells(x_ref[rows, :])
            g = 1.0 - f
            v = turned_pieces(
                cell,
                (
                    c * f * f,
                    c + f * (2.0 * c - 3.0 * c * f),
                    -c - g * (2.0 * c - 3.0 * c * g),
                    -c * g * g,
                ),
            )
            total = None
            for q in range(4):
                live = jnp.where(
                    cell < float(q + 4), wide_ref[block % 2, q, here], wide_ref[block % 2, q + 4, here]
                )
                term = v[q] * live
                total = term if total is None else total + term
            partial_ref[rows, :] = total.astype(bf16)
        copies.append(pltpu.make_async_copy(partial_ref.at[at], out_ref.at[at], sems.at[block]))
        copies[-1].start()
    for copy in copies:
        copy.wait()


def project(data, x, coefs, after):
    slots = data.shape[0]
    step = 256
    return pl.pallas_call(
        project_kernel,
        out_shape=(pltpu.HBM((slots, IN), bf16), TOKEN),
        in_specs=vmem(3) + [ANYWHERE],
        out_specs=(pl.BlockSpec(memory_space=pltpu.HBM), vmem(1)[0]),
        scratch_shapes=[
            pltpu.VMEM((2, NB, step, IN), f32),
            pltpu.VMEM((slots, IN), bf16),
            pltpu.SemaphoreType.DMA((slots // step,)),
        ],
        compiler_params=LIMIT,
        cost_estimate=pl.CostEstimate(flops=2200000000, bytes_accessed=8000000, transcendentals=0),
        name="project",
    )(data, x, coefs, after)


def fill_basis(basis_ref, x_ref, start, quarter):
    slots = x_ref.shape[1]
    c = 1.0 / 6.0
    high, wide = 16, 256
    for low in range(0, quarter, high):
        for left in range(0, slots, wide):
            rows = pl.ds(pl.multiple_of(start + low, high), high)
            cell, f = cells(x_ref[rows, left : left + wide])
            g = 1.0 - f
            v = turned_pieces(
                cell,
                (
                    c * f * f * f,
                    c + f * (0.5 + f * (0.5 - 0.5 * f)),
                    c + g * (0.5 + g * (0.5 - 0.5 * g)),
                    c * g * g * g,
                ),
            )
            for q in range(4):
                below = cell < float(q + 4)
                for k, value in (
                    (q, jnp.where(below, v[q], 0.0)),
                    (q + 4, jnp.where(below, 0.0, v[q])),
                ):
                    at = k * quarter + low
                    basis_ref[at : at + high, left : left + wide] = value.astype(bf16)


def bases_dot(basis_ref, turned_ref, data_ref, start, quarter):
    fill_basis(basis_ref, turned_ref, start, quarter)
    return jnp.dot(basis_ref[...], data_ref[:, 0:COLS], preferred_element_type=f32).reshape(
        NB, quarter, COLS
    )


def pair_kernel(
    place_ref, data_ref, other_ref, out_ref, last_ref, own_ref, x_ref, done_ref, turned_ref, basis_ref,
    piece_ref, keep_ref, sems,
):
    done_ref[...] = jnp.zeros_like(done_ref)
    core = place_ref[4]
    for half, x in ((core, data_ref[:, COLS:WIDTH]), (1 - core, other_ref[...])):
        rows = pl.ds(pl.multiple_of(half * HALF, HALF), HALF)
        turned_ref[rows, :] = jnp.transpose(x.astype(f32)).astype(bf16)
        x_ref[:, rows] = x
    quarter = out_ref.shape[2]
    for which, ref in ((2, keep_ref), (0, own_ref)):
        ref[...] = turned_ref[pl.ds(pl.multiple_of(place_ref[which] * quarter, quarter), quarter), :]
    copies = [pltpu.make_async_copy(keep_ref, last_ref, sems.at[2])]
    copies[0].start()
    for index, which in enumerate((1, 3)):
        piece_ref[index] = bases_dot(
            basis_ref.at[index], turned_ref, data_ref, place_ref[which] * quarter, quarter
        ).astype(bf16)
        copies.append(pltpu.make_async_copy(piece_ref.at[index], out_ref.at[index], sems.at[index]))
        copies[-1].start()
    for copy in copies:
        copy.wait()


def pair(place, data, other, quarter):
    slots = data.shape[0]
    return pl.pallas_call(
        pair_kernel,
        out_shape=(
            pltpu.HBM((2, NB, quarter, COLS), bf16),
            pltpu.HBM((quarter, slots), bf16),
            jax.ShapeDtypeStruct((quarter, slots), bf16),
            jax.ShapeDtypeStruct((slots, IN), bf16),
            TOKEN,
        ),
        in_specs=[SCALARS] + vmem(2),
        out_specs=(pl.BlockSpec(memory_space=pltpu.HBM),) * 2 + tuple(vmem(3)),
        scratch_shapes=[
            pltpu.VMEM((IN, slots), bf16),
            pltpu.VMEM((2, NB * quarter, slots), bf16),
            pltpu.VMEM((2, NB, quarter, COLS), bf16),
            pltpu.VMEM((quarter, slots), bf16),
            pltpu.SemaphoreType.DMA((3,)),
        ],
        compiler_params=LIMIT,
        cost_estimate=pl.CostEstimate(flops=1100000000, bytes_accessed=4000000, transcendentals=0),
        name="pair",
    )(place, data, other)


def last_kernel(turned_ref, data_ref, came_ref, after_ref, out_ref, done_ref, basis_ref):
    done_ref[...] = jnp.zeros_like(done_ref)
    quarter = out_ref.shape[1]
    piece = bases_dot(basis_ref, turned_ref, data_ref, 0, quarter)
    out_ref[...] = (piece + came_ref[1].astype(f32)).astype(bf16)


def last_piece(turned, data, came, after, quarter):
    slots = data.shape[0]
    return pl.pallas_call(
        last_kernel,
        out_shape=(jax.ShapeDtypeStruct((NB, quarter, COLS), bf16), TOKEN),
        in_specs=vmem(3) + [ANYWHERE],
        out_specs=tuple(vmem(2)),
        scratch_shapes=[pltpu.VMEM((NB * quarter, slots), bf16)],
        compiler_params=LIMIT,
        name="last_piece",
    )(turned, data, came, after)


def own_kernel(
    turned_ref, data_ref, came_ref, coef_ref, after_ref, out_ref, basis_ref, wide_ref
):
    quarter = out_ref.shape[0]
    piece = bases_dot(basis_ref, turned_ref, data_ref, 0, quarter)
    piece = piece + came_ref[0].astype(f32)
    for j in range(COLS // LANES):
        lanes = slice(j * LANES, (j + 1) * LANES)
        for k in range(NB):
            wide_ref[j, pl.ds(k, quarter, stride=NB), :] = piece[k, :, lanes]
        out_ref[:, :, lanes] = wide_ref[j].reshape(quarter, NB, LANES)
    rows = penalty_rows()
    for i in range(0, quarter, 4):
        c = coef_ref[i : i + 4].astype(f32)
        pen = c * rows[0]
        for turn, weight in zip((1, 2, NB - 2, NB - 1), rows[1:]):
            pen = pen + pltpu.roll(c, turn, 1) * weight
        out_ref[i : i + 4] = out_ref[i : i + 4] + pen


def own_piece(turned, data, came, coef, after):
    slots = data.shape[0]
    quarter = coef.shape[0]
    return pl.pallas_call(
        own_kernel,
        out_shape=jax.ShapeDtypeStruct(coef.shape, f32),
        in_specs=vmem(4) + [ANYWHERE],
        out_specs=vmem(1)[0],
        scratch_shapes=[
            pltpu.VMEM((NB * quarter, slots), bf16),
            pltpu.VMEM((COLS // LANES, NB * quarter, LANES), f32),
        ],
        compiler_params=LIMIT,
        name="own_piece",
    )(turned, data, came, coef, after)


def adam_kernel(
    last_ref, sum_ref, coef_ref, one_ref, two_ref, new_ref, one_out, two_out, done_ref, wide_ref
):
    done_ref[...] = jnp.zeros_like(done_ref)
    rows = coef_ref.shape[0]
    small = 4
    for j in range(COLS // LANES):
        lanes = slice(j * LANES, (j + 1) * LANES)
        for k in range(NB):
            wide_ref[j, pl.ds(k, rows, stride=NB), :] = last_ref[k, :, lanes].astype(f32)
    for low in range(0, rows, small):
        at = slice(low, low + small)
        grad = jnp.concatenate(
            [
                wide_ref[j, low * NB : (low + small) * NB].reshape(small, NB, LANES)
                for j in range(COLS // LANES)
            ],
            axis=2,
        )
        grad = grad + sum_ref[at]
        c = coef_ref[at].astype(f32)
        one = BETA_ONE * one_ref[at].astype(f32) + (1.0 - BETA_ONE) * grad
        two = BETA_TWO * two_ref[at].astype(f32) + (1.0 - BETA_TWO) * grad * grad
        scaled = two * (1.0 / BIAS_TWO)
        root = scaled * lax.rsqrt(scaled)
        update = one * (1.0 / BIAS_ONE) / (root + EPSILON)
        new_ref[at] = (c - LEARN_RATE * (update + WEIGHT_DECAY * c)).astype(bf16)
        one_out[at] = one.astype(bf16)
        two_out[at] = two.astype(bf16)


def adam(last, total, coef, one, two):
    quarter = coef.shape[0]
    return pl.pallas_call(
        adam_kernel,
        out_shape=tuple(jax.ShapeDtypeStruct(coef.shape, bf16) for _ in range(3)) + (TOKEN,),
        in_specs=vmem(5),
        out_specs=tuple(vmem(4)),
        scratch_shapes=[pltpu.VMEM((COLS // LANES, quarter * NB, LANES), f32)],
        compiler_params=LIMIT,
        name="adam",
    )(last, total, coef, one, two)


def combine_kernel(returned_ref, onehot_ref, after_ref, out_ref):
    experts = returned_ref.shape[0]
    total = returned_ref[:, 0].astype(f32)
    for s in range(1, SPLIT):
        total = total + returned_ref[:, s].astype(f32)
    total = total.astype(bf16).reshape(experts * CAP, IN)
    out_ref[...] = lax.dot_general(
        onehot_ref[...], total, (((0,), (0,)), ((), ())), preferred_element_type=f32
    ).astype(bf16)


def combine(returned, onehot, after):
    return pl.pallas_call(
        combine_kernel,
        out_shape=jax.ShapeDtypeStruct((ROWS, IN), bf16),
        in_specs=vmem(2) + [ANYWHERE],
        out_specs=vmem(1)[0],
        compiler_params=LIMIT,
        name="combine",
    )(returned, onehot, after)


def on_device(inputs, out_grad, route, coef, first_moment, second_moment):
    groups = lax.axis_size("expert")
    members = lax.axis_size("dp")
    experts = groups // SPLIT
    quarter = IN // members
    core = lax.axis_index("expert") % 2
    here = lax.axis_index("dp")
    place = jnp.stack([here, here ^ (1 + 2 * core), here ^ (3 - 2 * core), here ^ 2, core])

    def swap(value, masks):
        pairs = [
            (g * members + (m ^ masks[g % 2]), g * members + m)
            for g in range(groups)
            for m in range(members)
        ]
        return lax.ppermute(value, ("expert", "dp"), pairs)

    send, onehot = dispatch(route.reshape(1, ROWS), inputs, out_grad, experts)
    got = lax.all_to_all(
        send.reshape(groups, CAP, WIDTH), "expert", split_axis=0, concat_axis=0, tiled=True
    ).reshape(groups * CAP, WIDTH)

    own = prepare(coef[0])
    first_coef = swap(own, (1, 3))
    second_coef = swap(own, (3, 1))
    third_coef = swap(first_coef, (3, 1))
    coefs, done = assemble(place, own, first_coef, second_coef, third_coef)

    other = lax.ppermute(take(got, done), "expert", [(g ^ 1, g) for g in range(groups)])
    sent, last_x, own_x, x, done = pair(place, got, other, quarter)
    came = swap(sent, (1, 3))
    partial, done = project(got, x, coefs, done)
    returned = lax.all_to_all(
        partial.reshape(groups, CAP, IN), "expert", split_axis=0, concat_axis=0, tiled=True
    )
    sent_last, done = last_piece(last_x, got, came, done, quarter)
    last = swap(sent_last, (3, 1))
    total = own_piece(own_x, got, came, coef[0], done)
    new_coef, new_one, new_two, done = adam(
        last, total, coef[0], first_moment[0], second_moment[0]
    )
    input_grad = combine(returned.reshape(experts, SPLIT, CAP, IN), onehot, done)
    return input_grad, new_coef[None], new_one[None], new_two[None]


def solution(mesh):
    rows = P(("expert", "dp"), None)
    state = P("expert", "dp", None, None)
    return jax.shard_map(
        on_device,
        mesh=mesh,
        in_specs=(rows, rows, rows, state, state, state),
        out_specs=(rows, state, state, state),
        check_vma=False,
    )
```

```python
import functools

import jax
import jax.numpy as jnp
from jax import lax
from jax.experimental import pallas as pl
from jax.experimental.pallas import tpu as pltpu
from jax.sharding import PartitionSpec as P

IN = 256
NB = 8
SPLIT = 4
COLS = 512
CAP = 8
ROWS = 128
LANES = 128
HALF = IN // 2
WIDTH = COLS + HALF

PENALTY = 10.0
LEARN_RATE = 0.001
BETA_ONE = 0.9
BETA_TWO = 0.999
EPSILON = 1e-08
WEIGHT_DECAY = 0.1
BIAS_ONE = 0.999973438601112
BIAS_TWO = 0.0952078528855534
HALF_INV_SPACING = 0.625

f32 = jnp.float32
bf16 = jnp.bfloat16


LIMIT = pltpu.CompilerParams(vmem_limit_bytes=28 * 1024 * 1024)


SCALARS = pl.BlockSpec(memory_space=pltpu.SMEM)


ANYWHERE = pl.BlockSpec(memory_space=pl.ANY)


TOKEN = jax.ShapeDtypeStruct((8, LANES), jnp.float32)


def vmem(n):
    return [pl.BlockSpec(memory_space=pltpu.VMEM) for _ in range(n)]


def slot_matrix(route_row, slots):
    wide = jnp.broadcast_to(route_row.astype(f32), (ROWS, ROWS))
    tall = jnp.transpose(wide)
    earlier = lax.broadcasted_iota(jnp.int32, (ROWS, ROWS), 0) < lax.broadcasted_iota(
        jnp.int32, (ROWS, ROWS), 1
    )
    rank = jnp.sum(jnp.where((wide == tall) & earlier, 1.0, 0.0), axis=0, keepdims=True)
    slot = route_row * CAP + rank.astype(jnp.int32)
    hit = lax.broadcasted_iota(jnp.int32, (slots, ROWS), 0) == slot
    return jnp.where(hit, 1.0, 0.0).astype(bf16)


def dispatch_kernel(route_ref, inputs_ref, grads_ref, send_ref, onehot_ref):
    experts = send_ref.shape[0]
    onehot = slot_matrix(route_ref[...], experts * CAP)
    onehot_ref[...] = onehot
    sent = jnp.dot(onehot, inputs_ref[...], preferred_element_type=f32).astype(bf16)
    sent = sent.reshape(experts, CAP, IN)
    for s in range(SPLIT):
        block = jnp.dot(
            onehot, grads_ref[:, s * COLS : (s + 1) * COLS], preferred_element_type=f32
        ).astype(bf16)
        send_ref[:, s, :, 0:COLS] = block.reshape(experts, CAP, COLS)
        send_ref[:, s, :, COLS:WIDTH] = sent[:, :, (s % 2) * HALF : (s % 2 + 1) * HALF]


def dispatch(route_row, inputs, out_grad, experts):
    return pl.pallas_call(
        dispatch_kernel,
        out_shape=(
            jax.ShapeDtypeStruct((experts, SPLIT, CAP, WIDTH), bf16),
            jax.ShapeDtypeStruct((experts * CAP, ROWS), bf16),
        ),
        in_specs=vmem(3),
        out_specs=tuple(vmem(2)),
        name="dispatch",
    )(route_row, inputs, out_grad)


def prepare_kernel(coef_ref, out_ref, wide_ref):
    quarter = out_ref.shape[1]
    for j in range(COLS // LANES):
        at = slice(j * LANES, (j + 1) * LANES)
        wide_ref[j] = coef_ref[:, :, at].reshape(quarter * NB, LANES).astype(f32)
        for k in range(NB):
            out_ref[k, :, at] = wide_ref[j, pl.ds(k, quarter, stride=NB), :].astype(bf16)


def prepare(coef):
    quarter = coef.shape[0]
    return pl.pallas_call(
        prepare_kernel,
        out_shape=jax.ShapeDtypeStruct((NB, quarter, COLS), bf16),
        in_specs=vmem(1),
        out_specs=vmem(1)[0],
        scratch_shapes=[pltpu.VMEM((COLS // LANES, quarter * NB, LANES), f32)],
        compiler_params=LIMIT,
        name="prepare",
    )(coef)


def penalty_rows():
    k = lax.broadcasted_iota(jnp.int32, (1, NB, COLS), 1)

    def row(values):
        out = jnp.full((1, NB, COLS), float(values[0]), f32)
        for index in range(1, NB):
            if values[index] != values[0]:
                out = jnp.where(k == index, float(values[index]), out)
        return out * PENALTY

    return (
        row((1, 5, 6, 6, 6, 6, 5, 1)),
        row((0, -2, -4, -4, -4, -4, -4, -2)),
        row((0, 0, 1, 1, 1, 1, 1, 1)),
        row((1, 1, 1, 1, 1, 1, 0, 0)),
        row((-2, -4, -4, -4, -4, -4, -2, 0)),
    )


def cells(x):
    t = x.astype(f32) * 1.25 + 5.5
    cell = jnp.floor(t)
    return cell, t - cell


def turned_pieces(cell, pieces):
    whole = cell.astype(jnp.int32)
    odd = (whole & 1) == 1
    high = (whole & 2) == 2
    s0, s1, s2, s3 = pieces
    a = (
        jnp.where(odd, s1, s0),
        jnp.where(odd, s0, s3),
        jnp.where(odd, s3, s2),
        jnp.where(odd, s2, s1),
    )
    v = [jnp.where(high, a[q - 2], a[q]) for q in range(4)]
    v[0] = jnp.where(cell < 8.0, v[0], 0.0)
    v[1] = jnp.where((cell >= 1.0) & (cell < 9.0), v[1], 0.0)
    v[2] = jnp.where((cell >= 2.0) & (cell < 10.0), v[2], 0.0)
    v[3] = jnp.where(cell >= 3.0, v[3], 0.0)
    return v


def assemble_kernel(place_ref, own_ref, first_ref, second_ref, third_ref, out_ref, done_ref):
    done_ref[...] = jnp.zeros_like(done_ref)
    out_ref[place_ref[0]] = own_ref[...]
    out_ref[place_ref[1]] = first_ref[...]
    out_ref[place_ref[2]] = second_ref[...]
    out_ref[place_ref[3]] = third_ref[...]


def assemble(place, own, first, second, third):
    return pl.pallas_call(
        assemble_kernel,
        out_shape=(jax.ShapeDtypeStruct((4,) + own.shape, bf16), TOKEN),
        in_specs=[SCALARS] + vmem(4),
        out_specs=tuple(vmem(2)),
        compiler_params=LIMIT,
        name="assemble",
    )(place, own, first, second, third)


def take_kernel(data_ref, after_ref, out_ref):
    out_ref[...] = data_ref[:, COLS:WIDTH]


def take(data, after):
    return pl.pallas_call(
        take_kernel,
        out_shape=jax.ShapeDtypeStruct((data.shape[0], HALF), bf16),
        in_specs=vmem(1) + [ANYWHERE],
        out_specs=vmem(1)[0],
        compiler_params=LIMIT,
        name="take",
    )(data, after)


def project_kernel(data_ref, x_ref, coef_ref, after_ref, out_ref, done_ref, wide_ref, partial_ref, sems):
    done_ref[...] = jnp.zeros_like(done_ref)
    copies = []
    slots = data_ref.shape[0]
    step = wide_ref.shape[2]
    small = 32
    c = HALF_INV_SPACING
    for block in range(slots // step):
        at = slice(block * step, (block + 1) * step)
        for k in range(NB):
            weight = jnp.concatenate([coef_ref[q, k] for q in range(coef_ref.shape[0])], axis=0)
            wide_ref[block % 2, k] = lax.dot_general(
                data_ref[at, 0:COLS], weight, (((1,), (1,)), ((), ())), preferred_element_type=f32
            )
        for low in range(0, step, small):
            here = slice(low, low + small)
            rows = slice(block * step + low, block * step + low + small)
            cell, f = cells(x_ref[rows, :])
            g = 1.0 - f
            v = turned_pieces(
                cell,
                (
                    c * f * f,
                    c + f * (2.0 * c - 3.0 * c * f),
                    -c - g * (2.0 * c - 3.0 * c * g),
                    -c * g * g,
                ),
            )
            total = None
            for q in range(4):
                live = jnp.where(
                    cell < float(q + 4), wide_ref[block % 2, q, here], wide_ref[block % 2, q + 4, here]
                )
                term = v[q] * live
                total = term if total is None else total + term
            partial_ref[rows, :] = total.astype(bf16)
        copies.append(pltpu.make_async_copy(partial_ref.at[at], out_ref.at[at], sems.at[block]))
        copies[-1].start()
    for copy in copies:
        copy.wait()


def project(data, x, coefs, after):
    slots = data.shape[0]
    step = 256
    return pl.pallas_call(
        project_kernel,
        out_shape=(pltpu.HBM((slots, IN), bf16), TOKEN),
        in_specs=vmem(3) + [ANYWHERE],
        out_specs=(pl.BlockSpec(memory_space=pltpu.HBM), vmem(1)[0]),
        scratch_shapes=[
            pltpu.VMEM((2, NB, step, IN), f32),
            pltpu.VMEM((slots, IN), bf16),
            pltpu.SemaphoreType.DMA((slots // step,)),
        ],
        compiler_params=LIMIT,
        cost_estimate=pl.CostEstimate(flops=2200000000, bytes_accessed=8000000, transcendentals=0),
        name="project",
    )(data, x, coefs, after)


def fill_basis(basis_ref, x_ref, start, quarter):
    slots = x_ref.shape[1]
    c = 1.0 / 6.0
    high, wide = 16, 256
    for low in range(0, quarter, high):
        for left in range(0, slots, wide):
            rows = pl.ds(pl.multiple_of(start + low, high), high)
            cell, f = cells(x_ref[rows, left : left + wide])
            g = 1.0 - f
            v = turned_pieces(
                cell,
                (
                    c * f * f * f,
                    c + f * (0.5 + f * (0.5 - 0.5 * f)),
                    c + g * (0.5 + g * (0.5 - 0.5 * g)),
                    c * g * g * g,
                ),
            )
            for q in range(4):
                below = cell < float(q + 4)
                for k, value in (
                    (q, jnp.where(below, v[q], 0.0)),
                    (q + 4, jnp.where(below, 0.0, v[q])),
                ):
                    at = k * quarter + low
                    basis_ref[at : at + high, left : left + wide] = value.astype(bf16)


def bases_dot(basis_ref, turned_ref, data_ref, start, quarter):
    fill_basis(basis_ref, turned_ref, start, quarter)
    return jnp.dot(basis_ref[...], data_ref[:, 0:COLS], preferred_element_type=f32).reshape(
        NB, quarter, COLS
    )


def turn_kernel(data_ref, after_ref, out_ref):
    out_ref[...] = jnp.transpose(data_ref[:, COLS:WIDTH].astype(f32)).astype(bf16)


def turn(data, after):
    return pl.pallas_call(
        turn_kernel,
        out_shape=jax.ShapeDtypeStruct((HALF, data.shape[0]), bf16),
        in_specs=vmem(1) + [ANYWHERE],
        out_specs=vmem(1)[0],
        compiler_params=LIMIT,
        name="turn",
    )(data, after)


def pair_kernel(
    place_ref, data_ref, other_ref, half_ref, out_ref, last_ref, own_ref, x_ref, done_ref, turned_ref, basis_ref,
    piece_ref, keep_ref, sems,
):
    done_ref[...] = jnp.zeros_like(done_ref)
    core = place_ref[4]
    for half, x in ((core, data_ref[:, COLS:WIDTH]), (1 - core, other_ref[...])):
        rows = pl.ds(pl.multiple_of(half * HALF, HALF), HALF)
        x_ref[:, rows] = x
        if half is core:
            turned_ref[rows, :] = half_ref[...]
        else:
            turned_ref[rows, :] = jnp.transpose(x.astype(f32)).astype(bf16)
    quarter = out_ref.shape[2]
    for which, ref in ((2, keep_ref), (0, own_ref)):
        ref[...] = turned_ref[pl.ds(pl.multiple_of(place_ref[which] * quarter, quarter), quarter), :]
    copies = [pltpu.make_async_copy(keep_ref, last_ref, sems.at[2])]
    copies[0].start()
    for index, which in enumerate((1, 3)):
        piece_ref[index] = bases_dot(
            basis_ref.at[index], turned_ref, data_ref, place_ref[which] * quarter, quarter
        ).astype(bf16)
        copies.append(pltpu.make_async_copy(piece_ref.at[index], out_ref.at[index], sems.at[index]))
        copies[-1].start()
    for copy in copies:
        copy.wait()


def pair(place, data, other, half, quarter):
    slots = data.shape[0]
    return pl.pallas_call(
        pair_kernel,
        out_shape=(
            pltpu.HBM((2, NB, quarter, COLS), bf16),
            pltpu.HBM((quarter, slots), bf16),
            jax.ShapeDtypeStruct((quarter, slots), bf16),
            jax.ShapeDtypeStruct((slots, IN), bf16),
            TOKEN,
        ),
        in_specs=[SCALARS] + vmem(3),
        out_specs=(pl.BlockSpec(memory_space=pltpu.HBM),) * 2 + tuple(vmem(3)),
        scratch_shapes=[
            pltpu.VMEM((IN, slots), bf16),
            pltpu.VMEM((2, NB * quarter, slots), bf16),
            pltpu.VMEM((2, NB, quarter, COLS), bf16),
            pltpu.VMEM((quarter, slots), bf16),
            pltpu.SemaphoreType.DMA((3,)),
        ],
        compiler_params=LIMIT,
        cost_estimate=pl.CostEstimate(flops=1100000000, bytes_accessed=4000000, transcendentals=0),
        name="pair",
    )(place, data, other, half)


def last_kernel(turned_ref, data_ref, came_ref, after_ref, out_ref, done_ref, basis_ref):
    done_ref[...] = jnp.zeros_like(done_ref)
    quarter = out_ref.shape[1]
    piece = bases_dot(basis_ref, turned_ref, data_ref, 0, quarter)
    out_ref[...] = (piece + came_ref[1].astype(f32)).astype(bf16)


def last_piece(turned, data, came, after, quarter):
    slots = data.shape[0]
    return pl.pallas_call(
        last_kernel,
        out_shape=(jax.ShapeDtypeStruct((NB, quarter, COLS), bf16), TOKEN),
        in_specs=vmem(3) + [ANYWHERE],
        out_specs=tuple(vmem(2)),
        scratch_shapes=[pltpu.VMEM((NB * quarter, slots), bf16)],
        compiler_params=LIMIT,
        name="last_piece",
    )(turned, data, came, after)


def own_kernel(
    turned_ref, data_ref, came_ref, coef_ref, after_ref, out_ref, basis_ref, wide_ref
):
    quarter = out_ref.shape[0]
    piece = bases_dot(basis_ref, turned_ref, data_ref, 0, quarter)
    piece = piece + came_ref[0].astype(f32)
    for j in range(COLS // LANES):
        lanes = slice(j * LANES, (j + 1) * LANES)
        for k in range(NB):
            wide_ref[j, pl.ds(k, quarter, stride=NB), :] = piece[k, :, lanes]
        out_ref[:, :, lanes] = wide_ref[j].reshape(quarter, NB, LANES)
    rows = penalty_rows()
    for i in range(0, quarter, 4):
        c = coef_ref[i : i + 4].astype(f32)
        pen = c * rows[0]
        for turn, weight in zip((1, 2, NB - 2, NB - 1), rows[1:]):
            pen = pen + pltpu.roll(c, turn, 1) * weight
        out_ref[i : i + 4] = out_ref[i : i + 4] + pen


def own_piece(turned, data, came, coef, after):
    slots = data.shape[0]
    quarter = coef.shape[0]
    return pl.pallas_call(
        own_kernel,
        out_shape=jax.ShapeDtypeStruct(coef.shape, f32),
        in_specs=vmem(4) + [ANYWHERE],
        out_specs=vmem(1)[0],
        scratch_shapes=[
            pltpu.VMEM((NB * quarter, slots), bf16),
            pltpu.VMEM((COLS // LANES, NB * quarter, LANES), f32),
        ],
        compiler_params=LIMIT,
        name="own_piece",
    )(turned, data, came, coef, after)


def adam_kernel(
    last_ref, sum_ref, coef_ref, one_ref, two_ref, new_ref, one_out, two_out, done_ref, wide_ref
):
    done_ref[...] = jnp.zeros_like(done_ref)
    rows = coef_ref.shape[0]
    small = 4
    for j in range(COLS // LANES):
        lanes = slice(j * LANES, (j + 1) * LANES)
        for k in range(NB):
            wide_ref[j, pl.ds(k, rows, stride=NB), :] = last_ref[k, :, lanes].astype(f32)
    for low in range(0, rows, small):
        at = slice(low, low + small)
        grad = jnp.concatenate(
            [
                wide_ref[j, low * NB : (low + small) * NB].reshape(small, NB, LANES)
                for j in range(COLS // LANES)
            ],
            axis=2,
        )
        grad = grad + sum_ref[at]
        c = coef_ref[at].astype(f32)
        one = BETA_ONE * one_ref[at].astype(f32) + (1.0 - BETA_ONE) * grad
        two = BETA_TWO * two_ref[at].astype(f32) + (1.0 - BETA_TWO) * grad * grad
        scaled = two * (1.0 / BIAS_TWO)
        root = scaled * lax.rsqrt(scaled)
        update = one * (1.0 / BIAS_ONE) / (root + EPSILON)
        new_ref[at] = (c - LEARN_RATE * (update + WEIGHT_DECAY * c)).astype(bf16)
        one_out[at] = one.astype(bf16)
        two_out[at] = two.astype(bf16)


def adam(last, total, coef, one, two):
    quarter = coef.shape[0]
    return pl.pallas_call(
        adam_kernel,
        out_shape=tuple(jax.ShapeDtypeStruct(coef.shape, bf16) for _ in range(3)) + (TOKEN,),
        in_specs=vmem(5),
        out_specs=tuple(vmem(4)),
        scratch_shapes=[pltpu.VMEM((COLS // LANES, quarter * NB, LANES), f32)],
        compiler_params=LIMIT,
        name="adam",
    )(last, total, coef, one, two)


def combine_kernel(returned_ref, onehot_ref, after_ref, out_ref):
    experts = returned_ref.shape[0]
    total = returned_ref[:, 0].astype(f32)
    for s in range(1, SPLIT):
        total = total + returned_ref[:, s].astype(f32)
    total = total.astype(bf16).reshape(experts * CAP, IN)
    out_ref[...] = lax.dot_general(
        onehot_ref[...], total, (((0,), (0,)), ((), ())), preferred_element_type=f32
    ).astype(bf16)


def combine(returned, onehot, after):
    return pl.pallas_call(
        combine_kernel,
        out_shape=jax.ShapeDtypeStruct((ROWS, IN), bf16),
        in_specs=vmem(2) + [ANYWHERE],
        out_specs=vmem(1)[0],
        compiler_params=LIMIT,
        name="combine",
    )(returned, onehot, after)


def on_device(inputs, out_grad, route, coef, first_moment, second_moment):
    groups = lax.axis_size("expert")
    members = lax.axis_size("dp")
    experts = groups // SPLIT
    quarter = IN // members
    core = lax.axis_index("expert") % 2
    here = lax.axis_index("dp")
    place = jnp.stack([here, here ^ (1 + 2 * core), here ^ (3 - 2 * core), here ^ 2, core])

    def swap(value, masks):
        pairs = [
            (g * members + (m ^ masks[g % 2]), g * members + m)
            for g in range(groups)
            for m in range(members)
        ]
        return lax.ppermute(value, ("expert", "dp"), pairs)

    send, onehot = dispatch(route.reshape(1, ROWS), inputs, out_grad, experts)
    got = lax.all_to_all(
        send.reshape(groups, CAP, WIDTH), "expert", split_axis=0, concat_axis=0, tiled=True
    ).reshape(groups * CAP, WIDTH)

    own = prepare(coef[0])
    first_coef = swap(own, (1, 3))
    second_coef = swap(own, (3, 1))
    third_coef = swap(first_coef, (3, 1))
    coefs, done = assemble(place, own, first_coef, second_coef, third_coef)

    half = take(got, done)
    other = lax.ppermute(half, "expert", [(g ^ 1, g) for g in range(groups)])
    sent, last_x, own_x, x, done = pair(place, got, other, turn(got, half), quarter)
    came = swap(sent, (1, 3))
    partial, done = project(got, x, coefs, done)
    returned = lax.all_to_all(
        partial.reshape(groups, CAP, IN), "expert", split_axis=0, concat_axis=0, tiled=True
    )
    sent_last, done = last_piece(last_x, got, came, done, quarter)
    last = swap(sent_last, (3, 1))
    total = own_piece(own_x, got, came, coef[0], done)
    new_coef, new_one, new_two, done = adam(
        last, total, coef[0], first_moment[0], second_moment[0]
    )
    input_grad = combine(returned.reshape(experts, SPLIT, CAP, IN), onehot, done)
    return input_grad, new_coef[None], new_one[None], new_two[None]


def solution(mesh):
    rows = P(("expert", "dp"), None)
    state = P("expert", "dp", None, None)
    return jax.shard_map(
        on_device,
        mesh=mesh,
        in_specs=(rows, rows, rows, state, state, state),
        out_specs=(rows, state, state, state),
        check_vma=False,
    )
```
